32 devices in a mesh: cam: 4 (over y, core), tile: 8 (over z, x).
Axes of the slice: x: 2, y: 2, z: 4, core: 2. Of those that a mesh axis runs over, the one named last changes fastest.
Arguments:
- tokens: bfloat16 [5632, 1024], P(('cam', 'tile')), may hold values from -16 to 16
- ln_gain: float32 [1024], replicated, may hold values from 0.25 to 1.75
- gate_weight: bfloat16 [1024, 2730], P(('cam', 'tile')), may hold values from -0.1875 to 0.1875
- up_weight: bfloat16 [1024, 2730], P(('cam', 'tile')), may hold values from -0.1875 to 0.1875
- down_weight: bfloat16 [2730, 1024], P(None, ('cam', 'tile')), may hold values from -0.109375 to 0.109375
- head_gain: float32 [1024], replicated, may hold values from 0.25 to 1.75
- depth_weight: bfloat16 [1024, 64], replicated, may hold values from -24 to 24
- context_weight: bfloat16 [1024, 128], replicated, may hold values from -3 to 3
- slot_point: int32 [32, 8, 2503], P(('cam', 'tile')), may hold values from 0 to 11263, as said below
- slot_cell: int32 [32, 8, 2503], P(('cam', 'tile')), may hold values from 0 to 2047, as said below
- slot_count: int32 [32, 8], P(('cam', 'tile')), may hold values from 312 to 2503
- conv1_weight: bfloat16 [3, 3, 128, 128], replicated, may hold values from -0.1875 to 0.1875
- conv1_bias: float32 [128], replicated, may hold values from -1.5 to 1.5
- conv2_weight: bfloat16 [3, 3, 128, 128], replicated, may hold values from -0.1875 to 0.1875
- conv2_bias: float32 [128], replicated, may hold values from -1.5 to 1.5
Outputs:
- bev_out: bfloat16 [8, 32, 256, 128], P('cam', 'tile')
The draws below stay inside these ranges and needn't reach their ends.
Inputs may be any that keep to these rules, and one draw needn't show every extreme that they name: slot_point[s, d, k] is a point of source s; the live slots (k < slot_count[s, d]) of one source name distinct points. slot_cell[s, d, k] is a cell of tile d, numbered as in the reference program.
All inputs are finite; a program needn't handle non-finite values.
Results may differ from the reference program's by a relative error of at most 0.013.
The reference program's roundings to bfloat16 on the way count: a program that leaves them out, or rounds other values in their place, can miss the bound.
Values may be sent and summed in bfloat16 or wider, within the bound.
A program may use at most 64 MiB of HBM per device.

```python
import math
import jax
import jax.numpy as jnp
from jax import lax

D = 1024
FF = 2730
BINS = 64
CH = 128
TOK_DEV = 176
ROWS_DEV = 4
GRID_W = 256
SCN = 2
SOURCES = 32
TOKENS = 5632
SCENES = 8
GRID_H = 32
SLOT = 2503
N_CAM = 4
N_TILE = 8


def plan_slots(key):
    sources = N_CAM * N_TILE
    point_total = TOK_DEV * BINS
    busiest = jax.random.randint(jax.random.fold_in(key, 11), (N_CAM,), 0, N_TILE)
    busiest_src = jnp.repeat(busiest, N_TILE)
    loads = jax.random.randint(jax.random.fold_in(key, 12), (sources, N_TILE), SLOT // 8, SLOT // 2 + 1)
    tile_ids = jnp.arange(N_TILE, dtype=jnp.int32)
    counts = jnp.where(tile_ids[None, :] == busiest_src[:, None], SLOT, loads).astype(jnp.int32)
    offsets = jnp.cumsum(counts, axis=1) - counts
    source_keys = jax.random.split(jax.random.fold_in(key, 13), sources)
    orders = jax.vmap(lambda single: jax.random.permutation(single, point_total))(source_keys)
    places = (offsets[:, :, None] + jnp.arange(SLOT, dtype=jnp.int32)[None, None, :]) % point_total
    points = jnp.take_along_axis(orders, places.reshape(sources, -1), axis=1)
    return (counts, points.reshape(sources, N_TILE, SLOT).astype(jnp.int32))


def draw_slot_point(key, part):
    counts, points = plan_slots(key)
    return points


def draw_slot_count(key, part):
    counts, points = plan_slots(key)
    return counts


def draw_slot_cell(key, part):
    return jax.random.randint(jax.random.fold_in(key, 21), (N_CAM * N_TILE, N_TILE, SLOT), 0, SCN * ROWS_DEV * GRID_W).astype(jnp.int32)


def draw_tokens(key, part):
    row_scale = jnp.exp(jax.random.uniform(jax.random.fold_in(key, 31), (TOKENS, 1), jnp.float32, math.log(0.3), math.log(3.0)))
    col_scale = jnp.exp(jax.random.uniform(jax.random.fold_in(key, 32), (1, D), jnp.float32, math.log(0.3), math.log(3.0)))
    noise = jax.random.normal(jax.random.fold_in(key, 33), (TOKENS, D), jnp.float32)
    values = row_scale * col_scale * noise
    return jnp.clip(values, -16.0, 16.0).astype(jnp.bfloat16)


def draw_depth_weight(key, part):
    base = jax.random.normal(jax.random.fold_in(key, 41), (D, BINS), jnp.float32) / math.sqrt(D)
    return jnp.clip(base, -24.0, 24.0).astype(jnp.bfloat16)


def steps_of(key, shape, cuts, smallest, top_value):
    factor_of, own = 1.0, jax.random.fold_in(key, 6)
    for position, shards_of in cuts:
        draws = jnp.exp(jax.random.uniform(jax.random.fold_in(own, position), (shards_of,), jnp.float32, smallest / len(cuts), top_value / len(cuts)))
        factor_of = factor_of * jnp.repeat(draws, shape[position] // shards_of).reshape([-1 if axis == position else 1 for axis in range(len(shape))])
    return factor_of


def normal_values(rng, shape, width, most, shards=(), kind=jnp.bfloat16):
    level = steps_of(rng, shape, shards, -0.22, 0.18) if shards else 1.0
    drawn = jax.random.normal(rng, shape, jnp.float32) * width * level
    return jnp.minimum(jnp.maximum(drawn, -most), most).astype(kind)


def setup_inputs(seed: int = 0) -> dict:
    streams_of = jax.random.split(jax.random.key(seed), 16)
    tokens = draw_tokens(jax.random.fold_in(streams_of[15], 71), 0)
    ln_gain = jnp.clip(1.0 + 0.15 * jax.random.normal(streams_of[1], (D,), jnp.float32), 0.25, 1.75)
    gate_weight = normal_values(streams_of[2], (D, FF), D ** -0.5, 0.1875, ((0, 32),))
    up_weight = normal_values(streams_of[3], (D, FF), D ** -0.5, 0.1875, ((0, 32),))
    down_weight = normal_values(streams_of[4], (FF, D), FF ** -0.5, 0.109375, ((1, 32),))
    head_gain = jnp.clip(1.0 + 0.15 * jax.random.normal(streams_of[5], (D,), jnp.float32), 0.25, 1.75)
    depth_weight = draw_depth_weight(jax.random.fold_in(streams_of[15], 71), 0)
    context_weight = normal_values(streams_of[7], (D, CH), (D // 256) ** -0.5, 3.0)
    slot_point = draw_slot_point(jax.random.fold_in(streams_of[15], 71), 0)
    slot_cell = draw_slot_cell(jax.random.fold_in(streams_of[15], 71), 0)
    slot_count = draw_slot_count(jax.random.fold_in(streams_of[15], 71), 0)
    conv1_weight = normal_values(streams_of[11], (3, 3, CH, CH), (9 * CH) ** -0.5, 0.1875)
    conv1_bias = normal_values(streams_of[12], (CH,), 0.3, 1.5, (), jnp.float32)
    conv2_weight = normal_values(streams_of[13], (3, 3, CH, CH), (9 * CH) ** -0.5, 0.1875)
    conv2_bias = normal_values(streams_of[14], (CH,), 0.3, 1.5, (), jnp.float32)
    return {"tokens": tokens, "ln_gain": ln_gain, "gate_weight": gate_weight, "up_weight": up_weight, "down_weight": down_weight, "head_gain": head_gain, "depth_weight": depth_weight, "context_weight": context_weight, "slot_point": slot_point, "slot_cell": slot_cell, "slot_count": slot_count, "conv1_weight": conv1_weight, "conv1_bias": conv1_bias, "conv2_weight": conv2_weight, "conv2_bias": conv2_bias}


def layer_norm(values, gain):
    center = values - lax.optimization_barrier(jnp.mean(values, axis=-1, keepdims=True))
    spread = lax.optimization_barrier(jnp.mean(center * center, axis=-1, keepdims=True))
    return center * lax.rsqrt(spread + 1e-06) * gain

def conv_rows(extended, weight):
    scenes = extended.shape[0]
    out_rows = extended.shape[1] - 2
    columns = extended.shape[2]
    padded = jnp.pad(extended, ((0, 0), (0, 0), (1, 1), (0, 0)))
    total = jnp.zeros((scenes * out_rows * columns, weight.shape[3]), jnp.float32)
    for row_shift in range(3):
        for col_shift in range(3):
            window = padded[:, row_shift:row_shift + out_rows, col_shift:col_shift + columns, :]
            window = window.reshape(-1, weight.shape[2])
            total = total + jnp.dot(window, weight[row_shift, col_shift], preferred_element_type=jnp.float32)
    return total.reshape(scenes, out_rows, columns, weight.shape[3])

def lift_source(token_rows, ln_gain, gate_weight, up_weight, down_weight, head_gain, depth_weight, context_weight, points, counts):
    inputs = token_rows.astype(jnp.float32)
    normed = layer_norm(inputs, ln_gain).astype(jnp.bfloat16)
    gate_full = jnp.dot(normed, gate_weight, preferred_element_type=jnp.float32)
    up_full = jnp.dot(normed, up_weight, preferred_element_type=jnp.float32)
    hidden = (jax.nn.silu(gate_full) * up_full).astype(jnp.bfloat16)
    updated = inputs + jnp.dot(hidden, down_weight, preferred_element_type=jnp.float32)
    head_input = layer_norm(updated, head_gain).astype(jnp.bfloat16)
    logits = jnp.dot(head_input, depth_weight, preferred_element_type=jnp.float32)
    context = jnp.dot(head_input, context_weight, preferred_element_type=jnp.float32).astype(jnp.bfloat16)
    context = lax.optimization_barrier(context).astype(jnp.float32)
    depth = jax.nn.softmax(logits, axis=-1)
    point_ids = points.reshape(-1)
    live = (jnp.arange(SLOT, dtype=jnp.int32)[None, :] < counts[:, None]).reshape(-1)
    weight_live = jnp.where(live, depth.reshape(-1)[point_ids], 0.0)
    lifted = weight_live[:, None] * context[point_ids // BINS]
    return lifted

def scene_block(grid):
    scene = grid[None]
    extended = jnp.pad(scene, ((0, 0), (1, 1), (0, 0), (0, 0)))
    return (scene, extended)

def reference(tokens, ln_gain, gate_weight, up_weight, down_weight, head_gain, depth_weight, context_weight, slot_point, slot_cell, slot_count, conv1_weight, conv1_bias, conv2_weight, conv2_bias):
    cell_count = SCN * ROWS_DEV * GRID_W

    def one_source(source, accum):
        token_rows = lax.dynamic_slice_in_dim(tokens, source * TOK_DEV, TOK_DEV, 0)
        lifted = lift_source(token_rows, ln_gain, gate_weight, up_weight, down_weight, head_gain, depth_weight, context_weight, slot_point[source], slot_count[source])
        group = source // N_TILE
        flat_cells = (jnp.arange(N_TILE, dtype=jnp.int32)[:, None] * cell_count + slot_cell[source]).reshape(-1)
        return accum.at[group, flat_cells].add(lifted)
    accum = lax.fori_loop(0, SOURCES, one_source, jnp.zeros((N_CAM, N_TILE * cell_count, CH), jnp.float32))
    bev = accum.astype(jnp.bfloat16).reshape(N_CAM, N_TILE, SCN, ROWS_DEV, GRID_W, CH)
    bev = bev.transpose(0, 2, 1, 3, 4, 5).reshape(SCENES, GRID_H, GRID_W, CH)

    def convolve(grid):
        scene, extended = scene_block(grid)
        middle = jnp.maximum(conv_rows(extended, conv1_weight) + conv1_bias, 0.0).astype(jnp.bfloat16)
        middle_ext = jnp.pad(middle, ((0, 0), (1, 1), (0, 0), (0, 0)))
        result = scene.astype(jnp.float32) + conv_rows(middle_ext, conv2_weight) + conv2_bias
        return result.astype(jnp.bfloat16)[0]
    return lax.map(convolve, bev)
```

```python
import jax
import jax.numpy as jnp
from jax import lax
from jax.experimental import pallas as pl
from jax.experimental.pallas import tpu as pltpu
from jax.sharding import PartitionSpec as P

ROWS_DEV = 4
GRID_W = 256
SCN = 2


def extended_2(value, sides, width):
    for axis, dim in sides:
        size, length = (lax.axis_size(axis), value.shape[dim])
        up = [(i, (i + 1) % size) for i in range(size - 1)]
        down = [(j, i) for i, j in up]
        last = lax.slice_in_dim(value, length - width, length, axis=dim)
        leading = lax.slice_in_dim(value, 0, width, axis=dim)
        before = lax.ppermute(last, axis, up)
        after = lax.ppermute(leading, axis, down)
        value = jnp.concatenate([before, value, after], axis=dim)
    return value


def layer_norm(values, gain):
    center = values - jnp.mean(values, axis=-1, keepdims=True)
    spread = jnp.mean(center * center, axis=-1, keepdims=True)
    return center * lax.rsqrt(spread + 1e-06) * gain


def conv_rows(extended, weight):
    scenes = extended.shape[0]
    out_rows = extended.shape[1] - 2
    columns = extended.shape[2]
    padded = jnp.pad(extended, ((0, 0), (0, 0), (1, 1), (0, 0)))
    total = jnp.zeros((scenes * out_rows * columns, weight.shape[3]), jnp.float32)
    for row_shift in range(3):
        for col_shift in range(3):
            window = padded[:, row_shift : row_shift + out_rows, col_shift : col_shift + columns, :]
            window = window.reshape(-1, weight.shape[2])
            total = total + jnp.dot(
                window, weight[row_shift, col_shift], preferred_element_type=jnp.float32
            )
    return total.reshape(scenes, out_rows, columns, weight.shape[3])


CHUNK = 512


def splat_kernel(rows_ref, table_ref, out_ref):
    sources, _, slots = rows_ref.shape
    tokens = table_ref.shape[2]
    half, wide = out_ref.shape
    channels = wide // 2
    bins = table_ref.shape[1] - channels
    chunks = slots // CHUNK
    out_ref[...] = jnp.zeros_like(out_ref)

    def step(i, carry):
        source = i // chunks
        start = pl.multiple_of((i % chunks) * CHUNK, CHUNK)
        rows = rows_ref[source, :, pl.ds(start, CHUNK)]
        token, depth_bin, cell = rows[0:1], rows[1:2], rows[2:3]
        token_ids = lax.broadcasted_iota(jnp.int32, (tokens, CHUNK), 0)
        pick = jnp.where(token_ids == token, 1.0, 0.0).astype(jnp.bfloat16)
        got = jnp.dot(table_ref[source], pick, preferred_element_type=jnp.float32)
        bin_ids = lax.broadcasted_iota(jnp.int32, (bins, CHUNK), 0)
        weight = jnp.sum(
            jnp.where(bin_ids == depth_bin, got[:bins], 0.0), axis=0, keepdims=True
        )
        upper = cell >= half
        low = jnp.where(upper, 0.0, weight) * got[bins:]
        high = jnp.where(upper, weight, 0.0) * got[bins:]
        lifted = jnp.concatenate([low, high], axis=0).astype(jnp.bfloat16)
        local = jnp.where(upper, cell - half, cell)
        cell_ids = lax.broadcasted_iota(jnp.int32, (half, CHUNK), 0)
        place = jnp.where(cell_ids == local, 1.0, 0.0).astype(jnp.bfloat16)
        out_ref[...] += lax.dot_general(
            place, lifted, (((1,), (1,)), ((), ())), preferred_element_type=jnp.float32
        )
        return carry

    lax.fori_loop(0, sources * chunks, step, 0)


def splat_cells(rows, table, cell_count, channels):
    half = cell_count // 2
    out = pl.pallas_call(
        splat_kernel,
        out_shape=jax.ShapeDtypeStruct((half, 2 * channels), jnp.float32),
        in_specs=[pl.BlockSpec(memory_space=pltpu.VMEM)] * 2,
        out_specs=pl.BlockSpec(memory_space=pltpu.VMEM),
        compiler_params=pltpu.CompilerParams(vmem_limit_bytes=48 * 1024 * 1024),
        cost_estimate=pl.CostEstimate(
            flops=2 * cell_count * channels * rows.shape[0] * rows.shape[2],
            bytes_accessed=4 * cell_count * channels,
            transcendentals=0,
        ),
    )(rows, table)
    return jnp.concatenate([out[:, :channels], out[:, channels:]], axis=0)


def slot_rows(slot_point, slot_cell, slot_count, points, bins_count):
    tiles, slots = slot_point.shape[1:]
    live = jnp.arange(slots, dtype=jnp.int32)[None, :] < slot_count.reshape(tiles, 1)
    packed = jnp.where(live, slot_point.reshape(tiles, slots), points) * 65536
    packed = packed + slot_cell.reshape(tiles, slots)
    got = lax.all_to_all(packed, "tile", split_axis=0, concat_axis=0, tiled=True)
    got = jnp.pad(got, ((0, 0), (0, -slots % CHUNK)), constant_values=points * 65536)
    point = got // 65536
    zero = jnp.zeros_like(got)
    parts = [point // bins_count, point % bins_count, got % 65536]
    return jnp.stack(parts + [zero] * 5, axis=1)


def on_device(
    tokens,
    ln_gain,
    gate_weight,
    up_weight,
    down_weight,
    head_gain,
    depth_weight,
    context_weight,
    slot_point,
    slot_cell,
    slot_count,
    conv1_weight,
    conv1_bias,
    conv2_weight,
    conv2_bias,
):
    tiles = lax.axis_size("tile")
    token_count = tokens.shape[0]
    bins_count = depth_weight.shape[1]
    rows = slot_rows(slot_point, slot_cell, slot_count, token_count * bins_count, bins_count)
    inputs = tokens.astype(jnp.float32)
    normed = layer_norm(inputs, ln_gain).astype(jnp.bfloat16)
    gate_whole, up_whole = (
        lax.all_gather(gate_weight, ("cam", "tile"), axis=0, tiled=True),
        lax.all_gather(up_weight, ("cam", "tile"), axis=0, tiled=True),
    )
    gate_full = jnp.dot(normed, gate_whole, preferred_element_type=jnp.float32)
    up_full = jnp.dot(normed, up_whole, preferred_element_type=jnp.float32)
    hidden = (jax.nn.silu(gate_full) * up_full).astype(jnp.bfloat16)
    down_whole = lax.all_gather(down_weight.T, ("cam", "tile"), axis=0, tiled=True)
    branch_out = lax.dot_general(
        hidden, down_whole, (((1,), (1,)), ((), ())), preferred_element_type=jnp.float32
    )
    updated = inputs + branch_out
    head_input = layer_norm(updated, head_gain).astype(jnp.bfloat16)
    contract = (((0,), (1,)), ((), ()))
    logits = lax.dot_general(
        depth_weight, head_input, contract, preferred_element_type=jnp.float32
    )
    context = lax.dot_general(
        context_weight, head_input, contract, preferred_element_type=jnp.float32
    )
    depth = jax.nn.softmax(logits, axis=0)
    channels = context.shape[0]
    table = jnp.concatenate([depth, context], axis=0).astype(jnp.bfloat16)
    table_all = lax.all_gather(table, "tile", axis=0, tiled=False)
    cell_count = SCN * ROWS_DEV * GRID_W
    splat = splat_cells(rows, table_all, cell_count, channels)
    bev = splat.astype(jnp.bfloat16).reshape(SCN, ROWS_DEV, GRID_W, channels)
    extended = extended_2(bev, (("tile", 1),), 2)
    middle_wide = jnp.maximum(conv_rows(extended, conv1_weight) + conv1_bias, 0.0)
    global_rows = lax.axis_index("tile") * ROWS_DEV - 1 + jnp.arange(ROWS_DEV + 2, dtype=jnp.int32)
    inside = (global_rows >= 0) & (global_rows < tiles * ROWS_DEV)
    middle_ext = jnp.where(inside[None, :, None, None], middle_wide, 0.0).astype(jnp.bfloat16)
    result = bev.astype(jnp.float32) + conv_rows(middle_ext, conv2_weight) + conv2_bias
    return result.astype(jnp.bfloat16)


def solution(mesh):
    return jax.shard_map(
        on_device,
        mesh=mesh,
        in_specs=(
            P(("cam", "tile"), None),
            P(),
            P(("cam", "tile"), None),
            P(("cam", "tile"), None),
            P(None, ("cam", "tile")),
            P(),
            P(),
            P(),
            P(("cam", "tile"), None, None),
            P(("cam", "tile"), None, None),
            P(("cam", "tile"), None),
            P(),
            P(),
            P(),
            P(),
        ),
        out_specs=P("cam", "tile", None, None),
        check_vma=False,
    )
```

```python
import jax
import jax.numpy as jnp
from jax import lax
from jax.experimental import pallas as pl
from jax.experimental.pallas import tpu as pltpu
from jax.sharding import PartitionSpec as P

ROWS_DEV = 4
GRID_W = 256
SCN = 2


def extended_2(value, sides, width):
    for axis, dim in sides:
        size, length = (lax.axis_size(axis), value.shape[dim])
        up = [(i, (i + 1) % size) for i in range(size - 1)]
        down = [(j, i) for i, j in up]
        last = lax.slice_in_dim(value, length - width, length, axis=dim)
        leading = lax.slice_in_dim(value, 0, width, axis=dim)
        before = lax.ppermute(last, axis, up)
        after = lax.ppermute(leading, axis, down)
        value = jnp.concatenate([before, value, after], axis=dim)
    return value


def layer_norm(values, gain):
    center = values - jnp.mean(values, axis=-1, keepdims=True)
    spread = jnp.mean(center * center, axis=-1, keepdims=True)
    return center * lax.rsqrt(spread + 1e-06) * gain


def conv_rows(extended, weight):
    scenes = extended.shape[0]
    out_rows = extended.shape[1] - 2
    columns = extended.shape[2]
    padded = jnp.pad(extended, ((0, 0), (0, 0), (1, 1), (0, 0)))
    total = jnp.zeros((scenes * out_rows * columns, weight.shape[3]), jnp.float32)
    for row_shift in range(3):
        for col_shift in range(3):
            window = padded[:, row_shift : row_shift + out_rows, col_shift : col_shift + columns, :]
            window = window.reshape(-1, weight.shape[2])
            total = total + jnp.dot(
                window, weight[row_shift, col_shift], preferred_element_type=jnp.float32
            )
    return total.reshape(scenes, out_rows, columns, weight.shape[3])


CHUNK = 512


def splat_kernel(rows_ref, table_ref, out_ref, held, send_sem, recv_sem):
    tiles, _, slots = rows_ref.shape
    tokens = table_ref.shape[1]
    half, wide = out_ref.shape
    channels = wide // 2
    bins = table_ref.shape[0] - channels
    chunks = slots // CHUNK
    me = lax.axis_index("tile")

    def table_copy(k):
        return pltpu.make_async_remote_copy(
            src_ref=table_ref,
            dst_ref=held.at[k],
            send_sem=send_sem.at[k],
            recv_sem=recv_sem.at[k],
            device_id={"tile": lax.rem(me - k + tiles, tiles)},
            device_id_type=pl.DeviceIdType.MESH,
        )

    barrier = pltpu.get_barrier_semaphore()

    def greet(k, carry):
        other = lax.rem(me + k, tiles)
        pl.semaphore_signal(
            barrier, inc=1, device_id={"tile": other}, device_id_type=pl.DeviceIdType.MESH
        )
        return carry

    def send(k, carry):
        table_copy(k).start()
        return carry

    def finish(k, carry):
        table_copy(k).wait_send()
        return carry

    lax.fori_loop(1, tiles, greet, 0)
    pl.semaphore_wait(barrier, tiles - 1)
    lax.fori_loop(1, tiles, send, 0)
    out_ref[...] = jnp.zeros_like(out_ref)
    held[0] = table_ref[...]

    def one_source(k, carry):
        @pl.when(k > 0)
        def _():
            table_copy(k).wait_recv()

        source = lax.rem(me + k, tiles)

        def step(i, inner):
            start = pl.multiple_of(i * CHUNK, CHUNK)
            rows = rows_ref[source, :, pl.ds(start, CHUNK)]
            token, depth_bin, cell = rows[0:1], rows[1:2], rows[2:3]
            token_ids = lax.broadcasted_iota(jnp.int32, (tokens, CHUNK), 0)
            pick = jnp.where(token_ids == token, 1.0, 0.0).astype(jnp.bfloat16)
            got = jnp.dot(held[k], pick, preferred_element_type=jnp.float32)
            bin_ids = lax.broadcasted_iota(jnp.int32, (bins, CHUNK), 0)
            weight = jnp.sum(
                jnp.where(bin_ids == depth_bin, got[:bins], 0.0), axis=0, keepdims=True
            )
            upper = cell >= half
            low = jnp.where(upper, 0.0, weight) * got[bins:]
            high = jnp.where(upper, weight, 0.0) * got[bins:]
            lifted = jnp.concatenate([low, high], axis=0).astype(jnp.bfloat16)
            local = jnp.where(upper, cell - half, cell)
            cell_ids = lax.broadcasted_iota(jnp.int32, (half, CHUNK), 0)
            place = jnp.where(cell_ids == local, 1.0, 0.0).astype(jnp.bfloat16)
            out_ref[...] += lax.dot_general(
                place, lifted, (((1,), (1,)), ((), ())), preferred_element_type=jnp.float32
            )
            return inner

        return lax.fori_loop(0, chunks, step, carry)

    lax.fori_loop(0, tiles, one_source, 0)
    lax.fori_loop(1, tiles, finish, 0)


def splat_cells(rows, table, cell_count, channels):
    half = cell_count // 2
    tiles = rows.shape[0]
    out = pl.pallas_call(
        splat_kernel,
        out_shape=jax.ShapeDtypeStruct((half, 2 * channels), jnp.float32),
        in_specs=[pl.BlockSpec(memory_space=pltpu.VMEM)] * 2,
        out_specs=pl.BlockSpec(memory_space=pltpu.VMEM),
        scratch_shapes=[
            pltpu.VMEM((tiles, *table.shape), table.dtype),
            pltpu.SemaphoreType.DMA((tiles,)),
            pltpu.SemaphoreType.DMA((tiles,)),
        ],
        compiler_params=pltpu.CompilerParams(
            collective_id=0, has_side_effects=True, vmem_limit_bytes=48 * 1024 * 1024
        ),
        cost_estimate=pl.CostEstimate(
            flops=2 * cell_count * channels * tiles * rows.shape[2],
            bytes_accessed=4 * cell_count * channels,
            transcendentals=0,
        ),
    )(rows, table)
    return jnp.concatenate([out[:, :channels], out[:, channels:]], axis=0)


def slot_rows(slot_point, slot_cell, slot_count, points, bins_count):
    tiles, slots = slot_point.shape[1:]
    live = jnp.arange(slots, dtype=jnp.int32)[None, :] < slot_count.reshape(tiles, 1)
    packed = jnp.where(live, slot_point.reshape(tiles, slots), points) * 65536
    packed = packed + slot_cell.reshape(tiles, slots)
    got = lax.all_to_all(packed, "tile", split_axis=0, concat_axis=0, tiled=True)
    got = jnp.pad(got, ((0, 0), (0, -slots % CHUNK)), constant_values=points * 65536)
    point = got // 65536
    zero = jnp.zeros_like(got)
    parts = [point // bins_count, point % bins_count, got % 65536]
    return jnp.stack(parts + [zero] * 5, axis=1)


def on_device(
    tokens,
    ln_gain,
    gate_weight,
    up_weight,
    down_weight,
    head_gain,
    depth_weight,
    context_weight,
    slot_point,
    slot_cell,
    slot_count,
    conv1_weight,
    conv1_bias,
    conv2_weight,
    conv2_bias,
):
    tiles = lax.axis_size("tile")
    token_count = tokens.shape[0]
    bins_count = depth_weight.shape[1]
    rows = slot_rows(slot_point, slot_cell, slot_count, token_count * bins_count, bins_count)
    inputs = tokens.astype(jnp.float32)
    normed = layer_norm(inputs, ln_gain).astype(jnp.bfloat16)
    gate_whole, up_whole = (
        lax.all_gather(gate_weight, ("cam", "tile"), axis=0, tiled=True),
        lax.all_gather(up_weight, ("cam", "tile"), axis=0, tiled=True),
    )
    gate_full = jnp.dot(normed, gate_whole, preferred_element_type=jnp.float32)
    up_full = jnp.dot(normed, up_whole, preferred_element_type=jnp.float32)
    hidden = (jax.nn.silu(gate_full) * up_full).astype(jnp.bfloat16)
    down_whole = lax.all_gather(down_weight.T, ("cam", "tile"), axis=0, tiled=True)
    branch_out = lax.dot_general(
        hidden, down_whole, (((1,), (1,)), ((), ())), preferred_element_type=jnp.float32
    )
    updated = inputs + branch_out
    head_input = layer_norm(updated, head_gain).astype(jnp.bfloat16)
    contract = (((0,), (1,)), ((), ()))
    logits = lax.dot_general(
        depth_weight, head_input, contract, preferred_element_type=jnp.float32
    )
    context = lax.dot_general(
        context_weight, head_input, contract, preferred_element_type=jnp.float32
    )
    depth = jax.nn.softmax(logits, axis=0)
    channels = context.shape[0]
    table = jnp.concatenate([depth, context], axis=0).astype(jnp.bfloat16)
    cell_count = SCN * ROWS_DEV * GRID_W
    splat = splat_cells(rows, table, cell_count, channels)
    bev = splat.astype(jnp.bfloat16).reshape(SCN, ROWS_DEV, GRID_W, channels)
    extended = extended_2(bev, (("tile", 1),), 2)
    middle_wide = jnp.maximum(conv_rows(extended, conv1_weight) + conv1_bias, 0.0)
    global_rows = lax.axis_index("tile") * ROWS_DEV - 1 + jnp.arange(ROWS_DEV + 2, dtype=jnp.int32)
    inside = (global_rows >= 0) & (global_rows < tiles * ROWS_DEV)
    middle_ext = jnp.where(inside[None, :, None, None], middle_wide, 0.0).astype(jnp.bfloat16)
    result = bev.astype(jnp.float32) + conv_rows(middle_ext, conv2_weight) + conv2_bias
    return result.astype(jnp.bfloat16)


def solution(mesh):
    return jax.shard_map(
        on_device,
        mesh=mesh,
        in_specs=(
            P(("cam", "tile"), None),
            P(),
            P(("cam", "tile"), None),
            P(("cam", "tile"), None),
            P(None, ("cam", "tile")),
            P(),
            P(),
            P(),
            P(("cam", "tile"), None, None),
            P(("cam", "tile"), None, None),
            P(("cam", "tile"), None),
            P(),
            P(),
            P(),
            P(),
        ),
        out_specs=P("cam", "tile", None, None),
        check_vma=False,
    )
```
